512 devices in a mesh: obs: 16 (over z), src: 32 (over x, y, core).
Axes of the slice: x: 4, y: 4, z: 16, core: 2. Of those that a mesh axis runs over, the one named last changes fastest.
Arguments:
- delay_near: bfloat16 [16384, 16384], P('src', 'obs'), may hold values from -0.09375 to 0.09375
- delay_far: bfloat16 [16384, 16384], P('src', 'obs'), may hold values from -0.046875 to 0.046875
- incident: bfloat16 [4, 16384, 192], P(None, 'src'), may hold values from -6 to 6
- current_prev: bfloat16 [16384, 192], P('obs'), may hold values from -0.8984375 to 0.8984375
- current_prev2: bfloat16 [16384, 192], P('obs'), may hold values from -0.8984375 to 0.8984375
Outputs:
- currents: bfloat16 [4, 16384, 192], P(None, 'obs')
The draws below stay inside these ranges and needn't reach their ends.
All inputs are finite; a program needn't handle non-finite values.
Results may differ from the reference program's by a relative error of at most 0.003.
Values may be sent and summed in bfloat16 or wider, within the bound.
A program may use at most 64 MiB of HBM per device.

```python
import jax
import jax.numpy as jnp

N = 16384
R = 192
STEPS = 4


def spiked(result, key, source, target, parts, factor):
    owner, partner = [(jnp.arange(result.shape[dim]) // (result.shape[dim] // parts)).reshape([-1 if axis == dim else 1 for axis in range(result.ndim)]) for dim in (source, target)]
    chosen = jax.random.permutation(key, parts)[partner]
    strong = (owner == chosen) | (owner == (partner + parts // 2) % parts)
    return jnp.where(strong, factor * result, result)


def shard_levels(stream_key, dims, pieces, low, largest):
    gain = 1.0
    for position, shards_of in pieces:
        steps = jax.random.uniform(jax.random.fold_in(jax.random.fold_in(stream_key, 6), position), (shards_of,), jnp.float32, low / len(pieces), largest / len(pieces))
        gain = gain * jnp.repeat(jnp.exp(steps), dims[position] // shards_of).reshape((-1,) + (1,) * (len(dims) - 1 - position))
    return gain


def centred(rng, shape, scale, reach, shards=(), dtype=jnp.bfloat16):
    result = scale * jax.random.normal(rng, shape, jnp.float32)
    if shards:
        result = result * shard_levels(rng, shape, shards, -0.22, 0.18)
    return jnp.clip(result, -reach, reach).astype(dtype)


def heavy_noise(rng, shape, width, bound, cuts, heavy, kind=jnp.bfloat16):
    values = width * jax.random.normal(rng, shape, jnp.float32)
    if cuts:
        values = values * shard_levels(rng, shape, cuts, -0.22, 0.18)
    return jnp.clip(spiked(values, jax.random.fold_in(rng, 3), *heavy), -bound, bound).astype(kind)


def setup_inputs(seed: int = 0) -> dict:
    arg_keys = jax.random.split(jax.random.key(seed), 6)
    return {
        "delay_near": heavy_noise(arg_keys[0], (N, N), N ** -0.5, 0.09375, ((0, 32), (1, 16)), (1, 0, 32, 2.75)),
        "delay_far": centred(arg_keys[1], (N, N), N ** -0.5, 0.046875, ((0, 32), (1, 16))),
        "incident": centred(arg_keys[2], (STEPS, N, R), 1.0, 6.0, ((1, 32),)),
        "current_prev": jnp.clip(jax.random.uniform(arg_keys[3], (N, R), jnp.float32, -0.8984375, 0.8984375) * shard_levels(arg_keys[3], (N, R), ((0, 16),), -0.4, 0.0), -0.8984375, 0.8984375).astype(jnp.bfloat16),
        "current_prev2": jnp.clip(jax.random.uniform(arg_keys[4], (N, R), jnp.float32, -0.8984375, 0.8984375) * shard_levels(arg_keys[4], (N, R), ((0, 16),), -0.4, 0.0), -0.8984375, 0.8984375).astype(jnp.bfloat16),
    }


def reference(delay_near, delay_far, incident, current_prev, current_prev2):
    lagged = current_prev2
    latest = current_prev
    history = []
    for moment in range(STEPS):
        field_sum = jnp.dot(delay_near, latest, preferred_element_type=jnp.float32)
        field_sum = field_sum + jnp.dot(delay_far, lagged, preferred_element_type=jnp.float32)
        new_current = jnp.tanh(incident[moment].astype(jnp.float32) - field_sum).astype(jnp.bfloat16)
        history.append(new_current)
        lagged = latest
        latest = new_current
    return jnp.stack(history)
```

```python
import functools
import math

import jax
import jax.numpy as jnp
from jax import lax
from jax.experimental import pallas as pl
from jax.experimental.pallas import tpu as pltpu
from jax.sharding import PartitionSpec as P

BATCHES = 4
GROUP = 2
WIRE = jnp.float32
MESH = pl.DeviceIdType.MESH


def both(*conds):
    return functools.reduce(jnp.logical_and, conds)


def kernel(
    steps, nz, side, near_ref, far_ref, inc_ref, prev_ref, prev2_ref, out_ref,
    cur, acc, lag, snd, got, inct, z_send, z_recv, b_send, b_recv, out_sem,
):
    nb, rb, m = acc.shape
    z = lax.axis_index("obs")
    src = lax.axis_index("src")
    core = lax.rem(src, 2)
    chip = src // 2
    x, y = chip // side, lax.rem(chip, side)

    rel = lax.rem(z - chip + nz, nz)
    upper = rel <= nz // 2
    dist = jnp.where(upper, rel, nz - rel)
    arm = jnp.where(upper, nz // 2, nz - nz // 2 - 1)
    is_root = rel == 0
    hop = jnp.where(lax.rem(dist, GROUP) == 0, GROUP, lax.rem(dist, GROUP))
    parent_z = lax.rem(jnp.where(upper, z - hop, z + hop) + nz, nz)
    parent_slot = hop - 1 + jnp.where(both(jnp.logical_not(upper), dist == hop), GROUP, 0)
    is_leaf = both(jnp.logical_not(is_root), (lax.rem(dist, GROUP) != 0) | (dist + 1 > arm))
    is_joint = both(jnp.logical_not(is_root), jnp.logical_not(is_leaf))

    rx, ry = z // side, lax.rem(z, side)
    dx = lax.rem(x - rx + side, side)
    dy = lax.rem(y - ry + side, side)
    is_source = both(dx == 0, dy == 0)
    sibling = (z, chip * 2 + 1 - core)

    def in_plane(kx, ky):
        tx = lax.rem(x + kx, side)
        ty = lax.rem(y + ky, side)
        return (z, (tx * side + ty) * 2 + core)

    peers = [in_plane(k, 0) for k in range(1, side)]
    peers += [in_plane(0, k) for k in range(1, side)]
    peers += [sibling]
    reach = sorted({k % nz for k in range(-GROUP, GROUP + 1)} - {0})
    peers += [(lax.rem(z + k, nz), src) for k in reach]
    barrier = pltpu.get_barrier_semaphore()
    for peer in peers:
        pl.semaphore_signal(barrier, inc=1, device_id=peer, device_id_type=MESH)

    for index, ref in ((0, prev2_ref), (1, prev_ref)):
        whole = ref[...].astype(jnp.float32).T.astype(jnp.bfloat16)
        for b in range(nb):
            for h in range(2):
                cur[index, b, h] = whole[b * rb : (b + 1) * rb, h * m : (h + 1) * m]

    def dot(rows, ref, half):
        cols = pl.ds(pl.multiple_of(half * m, m), m)
        return lax.dot_general(
            rows, ref[:, cols], (((1,), (1,)), ((), ())), preferred_element_type=jnp.float32
        )

    def lagged(index, b):
        lag[b] = dot(cur[index, b, 0], far_ref, 0) + dot(cur[index, b, 1], far_ref, 1)

    for b in range(nb):
        lagged(0, b)

    @pl.when(is_root)
    def _():
        for t in range(steps):
            inct[t] = inc_ref[t].astype(jnp.float32).T.reshape(nb, rb, m)

    pl.semaphore_wait(barrier, len(peers))

    def up(t, b):
        return pltpu.make_async_remote_copy(
            src_ref=snd.at[t, b], dst_ref=got.at[t, b, parent_slot],
            send_sem=z_send.at[t, b], recv_sem=z_recv.at[t, b, parent_slot],
            device_id=(parent_z, src), device_id_type=MESH,
        )

    def down(t, b, which, device):
        return pltpu.make_async_remote_copy(
            src_ref=cur.at[t + 2, b, core], dst_ref=cur.at[t + 2, b, core],
            send_sem=b_send.at[t, b, which], recv_sem=b_recv.at[t, b, core],
            device_id=device, device_id_type=MESH,
        )

    def wait_block(t, b, half):
        pltpu.make_async_remote_copy(
            src_ref=cur.at[t + 2, b, half], dst_ref=cur.at[t + 2, b, half],
            send_sem=b_send.at[t, b, 0], recv_sem=b_recv.at[t, b, half],
            device_id=sibling, device_id_type=MESH,
        ).wait_recv()

    def second_level(b):
        odd = lax.rem(b, 2)
        across = jnp.where(odd == 0, dy, dx) == 0
        return across, [in_plane(k * odd, k * (1 - odd)) for k in range(1, side)]

    def first_level(b):
        odd = lax.rem(b, 2)
        return [in_plane(k * (1 - odd), k * odd) for k in range(1, side)]

    def relay(t, b, start):
        across, targets = second_level(b)

        @pl.when(across)
        def _():
            for k, target in enumerate(targets):
                copy = down(t, b, 1 + k, target)
                copy.start() if start else copy.wait_send()

        copy = down(t, b, 0, sibling)
        copy.start() if start else copy.wait_send()

    def source(t, b, start):
        for k, target in enumerate(first_level(b)):
            copy = down(t, b, side + k, target)
            copy.start() if start else copy.wait_send()

    def take_own(t, b):
        @pl.when(jnp.logical_not(is_source))
        def _():
            wait_block(t, b, core)
            relay(t, b, True)

    def ahead(t, b):
        @pl.when(t > 0)
        def _():
            take_own(t - 1, b)

        total = lag[b] + dot(cur[t + 1, b, core], near_ref, core)

        @pl.when(t > 0)
        def _():
            wait_block(t - 1, b, 1 - core)

        total = total + dot(cur[t + 1, b, 1 - core], near_ref, 1 - core)

        @pl.when(is_leaf)
        def _():
            snd[t, b] = total.astype(WIRE)
            up(t, b).start()

        @pl.when(jnp.logical_not(is_leaf))
        def _():
            acc[b] = total

    def wait_part(t, b, slot):
        pltpu.make_async_remote_copy(
            src_ref=snd.at[t, b], dst_ref=got.at[t, b, slot],
            send_sem=z_send.at[t, b], recv_sem=z_recv.at[t, b, slot],
            device_id=(parent_z, src), device_id_type=MESH,
        ).wait_recv()

    def behind(t, b):
        @pl.when(is_joint)
        def _():
            for k in range(GROUP):
                @pl.when(dist + k + 1 <= arm)
                def _():
                    wait_part(t, b, k)
                    acc[b] += got[t, b, k].astype(jnp.float32)

            snd[t, b] = acc[b].astype(WIRE)
            up(t, b).start()

        @pl.when(is_root)
        def _():
            total = acc[b]
            for k in range(GROUP):
                for lower, length in ((0, nz // 2), (1, nz - nz // 2 - 1)):
                    if k + 1 <= length:
                        wait_part(t, b, k + GROUP * lower)
                        total = total + got[t, b, k + GROUP * lower].astype(jnp.float32)
            cur[t + 2, b, core] = jnp.tanh(inct[t, b] - total).astype(jnp.bfloat16)
            source(t, b, True)
            relay(t, b, True)

    skew = jnp.where(is_leaf, 0, jnp.where(arm - dist <= 2, 1, nb))

    def out_copy(t):
        return pltpu.make_async_copy(cur.at[t + 2], out_ref.at[t], out_sem.at[t])

    def step(t, carry):
        def turn(j, carry):
            @pl.when(j < nb)
            def _():
                ahead(t, j)

            @pl.when(both(j >= skew, j - skew < nb))
            def _():
                behind(t, j - skew)

            return carry

        lax.fori_loop(0, 2 * nb, turn, 0)

        @pl.when(t > 0)
        def _():
            out_copy(t - 1).start()

        @pl.when(t < steps - 1)
        def _():
            def refill(b, carry):
                lagged(t + 1, b)
                return carry

            lax.fori_loop(0, nb, refill, 0)

        return carry

    lax.fori_loop(0, steps, step, 0)

    def finish(b, carry):
        take_own(steps - 1, b)
        wait_block(steps - 1, b, 1 - core)
        return carry

    lax.fori_loop(0, nb, finish, 0)
    out_copy(steps - 1).start()

    def drain(i, carry):
        t, b = i // nb, lax.rem(i, nb)
        relay(t, b, False)

        @pl.when(is_source)
        def _():
            source(t, b, False)

        @pl.when(jnp.logical_not(is_root))
        def _():
            up(t, b).wait_send()

        return carry

    lax.fori_loop(0, steps * nb, drain, 0)
    for t in range(steps):
        out_copy(t).wait()


def per_device(delay_near, delay_far, incident, current_prev, current_prev2):
    steps, m, r = incident.shape
    nz = lax.axis_size("obs")
    side = math.isqrt(lax.axis_size("src") // 2)
    nb = BATCHES
    rb = r // nb
    vmem = pl.BlockSpec(memory_space=pltpu.VMEM)
    blocks = pl.pallas_call(
        functools.partial(kernel, steps, nz, side),
        out_shape=jax.ShapeDtypeStruct((steps, nb, 2, rb, m), jnp.bfloat16),
        in_specs=[vmem] * 5,
        out_specs=pl.BlockSpec(memory_space=pl.ANY),
        scratch_shapes=[
            pltpu.VMEM((steps + 2, nb, 2, rb, m), jnp.bfloat16),
            pltpu.VMEM((nb, rb, m), jnp.float32),
            pltpu.VMEM((nb, rb, m), jnp.float32),
            pltpu.VMEM((steps, nb, rb, m), WIRE),
            pltpu.VMEM((steps, nb, 2 * GROUP, rb, m), WIRE),
            pltpu.VMEM((steps, nb, rb, m), jnp.float32),
            pltpu.SemaphoreType.DMA((steps, nb)),
            pltpu.SemaphoreType.DMA((steps, nb, 2 * GROUP)),
            pltpu.SemaphoreType.DMA((steps, nb, 2 * side)),
            pltpu.SemaphoreType.DMA((steps, nb, 2)),
            pltpu.SemaphoreType.DMA((steps,)),
        ],
        compiler_params=pltpu.CompilerParams(collective_id=0, has_side_effects=True),
    )(delay_near, delay_far, incident, current_prev, current_prev2)
    return blocks.transpose(0, 2, 4, 1, 3).reshape(steps, 2 * m, r)


def solution(mesh):
    in_specs = (
        P("src", "obs"),
        P("src", "obs"),
        P(None, "src", None),
        P("obs", None),
        P("obs", None),
    )
    out_specs = P(None, "obs", None)
    return jax.shard_map(
        per_device, mesh=mesh, in_specs=in_specs, out_specs=out_specs, check_vma=False
    )
```

```python
import functools
import math

import jax
import jax.numpy as jnp
from jax import lax
from jax.experimental import pallas as pl
from jax.experimental.pallas import tpu as pltpu
from jax.sharding import PartitionSpec as P

BATCHES = 12
TOGETHER = 2
NEAR, FAR = 2, 6
SKEW = 3
MESH = pl.DeviceIdType.MESH


def both(*conds):
    return functools.reduce(jnp.logical_and, conds)


def coded(v):
    return (v * v * v * jnp.abs(v)).astype(jnp.bfloat16)


def decoded(c):
    c = c.astype(jnp.float32)
    size = lax.rsqrt(lax.rsqrt(jnp.abs(c) + 1e-36))
    return jnp.where(c < 0, -size, size)


def kernel(
    steps, nz, side, near_ref, far_ref, inc_ref, prev_ref, prev2_ref, out_ref,
    near, far, inct, cur, acc, lag, snd, got, z_send, z_recv, b_send, b_recv, in_sem, out_sem,
):
    nb, rb, m = acc.shape
    z = lax.axis_index("obs")
    src = lax.axis_index("src")
    core = lax.rem(src, 2)
    chip = src // 2
    x, y = chip // side, lax.rem(chip, side)

    rel = lax.rem(z - chip + nz, nz)
    upper = rel <= nz // 2
    dist = jnp.where(upper, rel, nz - rel)
    arm = jnp.where(upper, nz // 2, nz - nz // 2 - 1)
    is_root = rel == 0
    home = jnp.where(dist <= NEAR + 1, NEAR, FAR)
    apart = dist - home
    is_joint = both(jnp.logical_not(is_root), apart == 0)
    is_leaf = both(jnp.logical_not(is_root), apart != 0)
    to_root = (apart == 0) | (home > arm)
    hop = jnp.where(to_root, dist, apart)
    parent_z = lax.rem(jnp.where(upper, z - hop, z + hop) + nz, nz)
    root_slot = jnp.where(home == FAR, 0, 1) + jnp.where(upper, 0, 2)
    parent_slot = jnp.where(to_root, root_slot, jnp.where(apart > 0, 2 - apart, 1 - apart))

    rx, ry = z // side, lax.rem(z, side)
    dx = lax.rem(x - rx + side, side)
    dy = lax.rem(y - ry + side, side)
    is_source = both(dx == 0, dy == 0)
    sibling = (z, chip * 2 + 1 - core)

    def in_plane(kx, ky):
        tx = lax.rem(x + kx, side)
        ty = lax.rem(y + ky, side)
        return (z, (tx * side + ty) * 2 + core)

    peers = [in_plane(k, 0) for k in range(1, side)]
    peers += [in_plane(0, k) for k in range(1, side)]
    peers += [sibling]
    reach = sorted({k % nz for k in (-FAR, -2, -1, 1, 2, FAR)} - {0})
    peers += [(lax.rem(z + k, nz), src) for k in reach]
    barrier = pltpu.get_barrier_semaphore()
    for peer in peers:
        pl.semaphore_signal(barrier, inc=1, device_id=peer, device_id_type=MESH)

    def halves(ref, index):
        return [(ref.at[:, :, h * m : (h + 1) * m], cur.at[index, :, h]) for h in range(2)]

    loads = [(far_ref, far), *halves(prev2_ref, 0), (near_ref, near), *halves(prev_ref, 1)]
    loads = [pltpu.make_async_copy(*pair, in_sem.at[i]) for i, pair in enumerate(loads)]
    inc_load = pltpu.make_async_copy(inc_ref, inct, in_sem.at[6])
    for load in loads:
        load.start()

    @pl.when(is_root)
    def _():
        inc_load.start()

    k = TOGETHER

    def dot(index, group, ref, half):
        rows = cur[index, pl.ds(group * k, k), half].reshape(k * rb, m)
        cols = pl.ds(pl.multiple_of(half * m, m), m)
        field = lax.dot_general(
            rows, ref[:, cols], (((1,), (1,)), ((), ())), preferred_element_type=jnp.float32
        )
        return field.reshape(k, rb, m)

    def lagged(index, group):
        lag[pl.ds(group * k, k)] = dot(index, group, far, 0) + dot(index, group, far, 1)

    for load in loads[:3]:
        load.wait()
    for group in range(nb // k):
        lagged(0, group)
    for load in loads[3:]:
        load.wait()

    @pl.when(is_root)
    def _():
        inc_load.wait()

    pl.semaphore_wait(barrier, len(peers))

    def up(t, b):
        return pltpu.make_async_remote_copy(
            src_ref=snd.at[t, b], dst_ref=got.at[t, b, parent_slot],
            send_sem=z_send.at[t, b], recv_sem=z_recv.at[t, b, parent_slot],
            device_id=(parent_z, src), device_id_type=MESH,
        )

    def down(t, b, which, device):
        return pltpu.make_async_remote_copy(
            src_ref=cur.at[t + 2, b, core], dst_ref=cur.at[t + 2, b, core],
            send_sem=b_send.at[t, b, which], recv_sem=b_recv.at[t, b, core],
            device_id=device, device_id_type=MESH,
        )

    def wait_block(t, b, half):
        pltpu.make_async_remote_copy(
            src_ref=cur.at[t + 2, b, half], dst_ref=cur.at[t + 2, b, half],
            send_sem=b_send.at[t, b, 0], recv_sem=b_recv.at[t, b, half],
            device_id=sibling, device_id_type=MESH,
        ).wait_recv()

    def second_level(b):
        odd = lax.rem(b, 2)
        across = jnp.where(odd == 0, dy, dx) == 0
        return across, [in_plane(k * odd, k * (1 - odd)) for k in range(1, side)]

    def first_level(b):
        odd = lax.rem(b, 2)
        return [in_plane(k * (1 - odd), k * odd) for k in range(1, side)]

    def relay(t, b, start):
        across, targets = second_level(b)

        @pl.when(across)
        def _():
            for k, target in enumerate(targets):
                copy = down(t, b, 1 + k, target)
                copy.start() if start else copy.wait_send()

        copy = down(t, b, 0, sibling)
        copy.start() if start else copy.wait_send()

    def source(t, b, start):
        for k, target in enumerate(first_level(b)):
            copy = down(t, b, side + k, target)
            copy.start() if start else copy.wait_send()

    def take_own(t, b):
        @pl.when(jnp.logical_not(is_source))
        def _():
            wait_block(t, b, core)
            relay(t, b, True)

    def ahead(t, b):
        @pl.when(t > 0)
        def _():
            take_own(t - 1, b)

        @pl.when(lax.rem(b, k) == k - 1)
        def _():
            multiply(t, b // k)

    def multiply(t, group):
        mine = pl.ds(group * k, k)
        total = lag[mine] + dot(t + 1, group, near, core)

        @pl.when(t > 0)
        def _():
            for i in range(k):
                wait_block(t - 1, group * k + i, 1 - core)

        total = total + dot(t + 1, group, near, 1 - core)

        @pl.when(is_leaf)
        def _():
            snd[t, mine] = coded(total)
            for i in range(k):
                up(t, group * k + i).start()

        @pl.when(jnp.logical_not(is_leaf))
        def _():
            acc[mine] = total

    def wait_part(t, b, slot):
        pltpu.make_async_remote_copy(
            src_ref=snd.at[t, b], dst_ref=got.at[t, b, slot],
            send_sem=z_send.at[t, b], recv_sem=z_recv.at[t, b, slot],
            device_id=(parent_z, src), device_id_type=MESH,
        ).wait_recv()

    def behind(t, b):
        @pl.when(is_joint)
        def _():
            for slot, offset in enumerate((2, 1, -1, -2)):
                child = dist + offset

                @pl.when(both(child <= arm, (home == FAR) | (abs(offset) == 1)))
                def _(slot=slot):
                    wait_part(t, b, slot)
                    acc[b] += decoded(got[t, b, slot])

            snd[t, b] = coded(acc[b])
            up(t, b).start()

        @pl.when(is_root)
        def _():
            total = acc[b]
            for slot, least in ((1, 1), (0, FAR), (3, 1), (2, FAR)):
                if least <= (nz // 2 if slot < 2 else nz - nz // 2 - 1):
                    wait_part(t, b, slot)
                    total = total + decoded(got[t, b, slot])
            cur[t + 2, b, core] = jnp.tanh(inct[t, b].astype(jnp.float32) - total).astype(jnp.bfloat16)
            source(t, b, True)
            relay(t, b, True)

    skew = jnp.where(is_leaf, 0, jnp.where(is_root, nb, SKEW))

    def out_copies(t):
        return [
            pltpu.make_async_copy(
                cur.at[t + 2, :, h], out_ref.at[t, :, :, h * m : (h + 1) * m], out_sem.at[t, h]
            )
            for h in range(2)
        ]

    def step(t, carry):
        def turn(j, carry):
            @pl.when(j < nb)
            def _():
                ahead(t, j)

            @pl.when(both(j >= skew, j - skew < nb))
            def _():
                behind(t, j - skew)

            return carry

        lax.fori_loop(0, 2 * nb, turn, 0)

        @pl.when(t > 0)
        def _():
            for copy in out_copies(t - 1):
                copy.start()

        @pl.when(t < steps - 1)
        def _():
            def refill(group, carry):
                lagged(t + 1, group)
                return carry

            lax.fori_loop(0, nb // k, refill, 0)

        return carry

    lax.fori_loop(0, steps, step, 0)

    def finish(b, carry):
        take_own(steps - 1, b)
        wait_block(steps - 1, b, 1 - core)
        return carry

    lax.fori_loop(0, nb, finish, 0)
    for copy in out_copies(steps - 1):
        copy.start()

    def drain(i, carry):
        t, b = i // nb, lax.rem(i, nb)
        relay(t, b, False)

        @pl.when(is_source)
        def _():
            source(t, b, False)

        @pl.when(jnp.logical_not(is_root))
        def _():
            up(t, b).wait_send()

        return carry

    lax.fori_loop(0, steps * nb, drain, 0)
    for t in range(steps):
        for copy in out_copies(t):
            copy.wait()


def per_device(delay_near, delay_far, incident, current_prev, current_prev2):
    steps, m, r = incident.shape
    nz = lax.axis_size("obs")
    side = math.isqrt(lax.axis_size("src") // 2)
    nb = BATCHES
    rb = r // nb
    rows = (nb, rb, 2 * m)
    blocks = pl.pallas_call(
        functools.partial(kernel, steps, nz, side),
        out_shape=jax.ShapeDtypeStruct((steps, *rows), jnp.bfloat16),
        in_specs=[pl.BlockSpec(memory_space=pl.ANY)] * 5,
        out_specs=pl.BlockSpec(memory_space=pl.ANY),
        scratch_shapes=[
            pltpu.VMEM((m, 2 * m), jnp.bfloat16),
            pltpu.VMEM((m, 2 * m), jnp.bfloat16),
            pltpu.VMEM((steps, nb, rb, m), jnp.bfloat16),
            pltpu.VMEM((steps + 2, nb, 2, rb, m), jnp.bfloat16),
            pltpu.VMEM((nb, rb, m), jnp.float32),
            pltpu.VMEM((nb, rb, m), jnp.float32),
            pltpu.VMEM((steps, nb, rb, m), jnp.bfloat16),
            pltpu.VMEM((steps, nb, 4, rb, m), jnp.bfloat16),
            pltpu.SemaphoreType.DMA((steps, nb)),
            pltpu.SemaphoreType.DMA((steps, nb, 4)),
            pltpu.SemaphoreType.DMA((steps, nb, 2 * side)),
            pltpu.SemaphoreType.DMA((steps, nb, 2)),
            pltpu.SemaphoreType.DMA((7,)),
            pltpu.SemaphoreType.DMA((steps, 2)),
        ],
        compiler_params=pltpu.CompilerParams(collective_id=0, has_side_effects=True),
    )(
        delay_near,
        delay_far,
        incident.transpose(0, 2, 1).reshape(steps, nb, rb, m),
        current_prev.T.reshape(rows),
        current_prev2.T.reshape(rows),
    )
    return blocks.reshape(steps, r, 2 * m).transpose(0, 2, 1)


def solution(mesh):
    in_specs = (
        P("src", "obs"),
        P("src", "obs"),
        P(None, "src", None),
        P("obs", None),
        P("obs", None),
    )
    out_specs = P(None, "obs", None)
    return jax.shard_map(
        per_device, mesh=mesh, in_specs=in_specs, out_specs=out_specs, check_vma=False
    )
```

```python
import functools
import math

import jax
import jax.numpy as jnp
from jax import lax
from jax.experimental import pallas as pl
from jax.experimental.pallas import tpu as pltpu
from jax.sharding import PartitionSpec as P

BATCHES = 12
TOGETHER = 1
NEAR, FAR = 2, 6
SKEW = 2
VMEM = 60 * 1024 * 1024
LEAD = 1
MESH = pl.DeviceIdType.MESH


def both(*conds):
    return functools.reduce(jnp.logical_and, conds)


def coded(v):
    return (v * v * v * jnp.abs(v)).astype(jnp.bfloat16)


def decoded(c):
    c = c.astype(jnp.float32)
    size = lax.rsqrt(lax.rsqrt(jnp.abs(c) + 1e-36))
    return jnp.where(c < 0, -size, size)


def kernel(
    steps, nz, side, near_ref, far_ref, inc_ref, prev_ref, prev2_ref, out_ref,
    near, far, inct, cur, acc, lag, snd, got, z_send, z_recv, b_send, b_recv, in_sem, out_sem,
):
    nb, rb, m = acc.shape
    z = lax.axis_index("obs")
    src = lax.axis_index("src")
    core = lax.rem(src, 2)
    chip = src // 2
    x, y = chip // side, lax.rem(chip, side)

    rel = lax.rem(z - chip + nz, nz)
    upper = rel <= nz // 2
    dist = jnp.where(upper, rel, nz - rel)
    arm = jnp.where(upper, nz // 2, nz - nz // 2 - 1)
    is_root = rel == 0
    home = jnp.where(dist <= NEAR + 1, NEAR, FAR)
    apart = dist - home
    is_joint = both(jnp.logical_not(is_root), apart == 0)
    is_leaf = both(jnp.logical_not(is_root), apart != 0)
    to_root = (apart == 0) | (home > arm)
    hop = jnp.where(to_root, dist, apart)
    parent_z = lax.rem(jnp.where(upper, z - hop, z + hop) + nz, nz)
    root_slot = jnp.where(home == FAR, 0, 1) + jnp.where(upper, 0, 2)
    parent_slot = jnp.where(to_root, root_slot, jnp.where(apart > 0, 2 - apart, 1 - apart))

    rx, ry = z // side, lax.rem(z, side)
    dx = lax.rem(x - rx + side, side)
    dy = lax.rem(y - ry + side, side)
    is_source = both(dx == 0, dy == 0)
    sibling = (z, chip * 2 + 1 - core)

    far_first = sorted(range(1, side), key=lambda k: -min(k, side - k))

    def in_plane(kx, ky, which):
        tx = lax.rem(x + kx, side)
        ty = lax.rem(y + ky, side)
        return (z, (tx * side + ty) * 2 + which)

    peers = [in_plane(k, 0, c) for k in far_first for c in range(2)]
    peers += [in_plane(0, k, c) for k in far_first for c in range(2)]
    peers += [sibling]
    reach = sorted({k % nz for k in (-FAR, -2, -1, 1, 2, FAR)} - {0})
    peers += [(lax.rem(z + k, nz), src) for k in reach]
    barrier = pltpu.get_barrier_semaphore()
    for peer in peers:
        pl.semaphore_signal(barrier, inc=1, device_id=peer, device_id_type=MESH)

    def halves(ref, index):
        return [(ref.at[:, :, h * m : (h + 1) * m], cur.at[index, :, h]) for h in range(2)]

    loads = [(far_ref, far), *halves(prev2_ref, 0), (near_ref, near), *halves(prev_ref, 1)]
    loads = [pltpu.make_async_copy(*pair, in_sem.at[i]) for i, pair in enumerate(loads)]
    inc_load = pltpu.make_async_copy(inc_ref, inct, in_sem.at[6])
    for load in loads:
        load.start()

    @pl.when(is_root)
    def _():
        inc_load.start()

    k = TOGETHER

    def dot(index, group, ref, half):
        rows = cur[index, pl.ds(group * k, k), half].reshape(k * rb, m)
        cols = pl.ds(pl.multiple_of(half * m, m), m)
        field = lax.dot_general(
            rows, ref[:, cols], (((1,), (1,)), ((), ())), preferred_element_type=jnp.float32
        )
        return field.reshape(k, rb, m)

    def lagged(index, group):
        lag[pl.ds(group * k, k)] = dot(index, group, far, 0) + dot(index, group, far, 1)

    for load in loads[:3]:
        load.wait()
    for group in range(nb // k):
        lagged(0, group)
    for load in loads[3:]:
        load.wait()

    @pl.when(is_root)
    def _():
        inc_load.wait()

    pl.semaphore_wait(barrier, len(peers))

    def up(t, b):
        return pltpu.make_async_remote_copy(
            src_ref=snd.at[t, b], dst_ref=got.at[t, b, parent_slot],
            send_sem=z_send.at[t, b], recv_sem=z_recv.at[t, b, parent_slot],
            device_id=(parent_z, src), device_id_type=MESH,
        )

    def down(t, b, which, device):
        return pltpu.make_async_remote_copy(
            src_ref=cur.at[t + 2, b, core], dst_ref=cur.at[t + 2, b, core],
            send_sem=b_send.at[t, b, which], recv_sem=b_recv.at[t, b, core],
            device_id=device, device_id_type=MESH,
        )

    def wait_block(t, b, half):
        pltpu.make_async_remote_copy(
            src_ref=cur.at[t + 2, b, half], dst_ref=cur.at[t + 2, b, half],
            send_sem=b_send.at[t, b, 0], recv_sem=b_recv.at[t, b, half],
            device_id=sibling, device_id_type=MESH,
        ).wait_recv()

    def place(b):
        odd = lax.rem(b, 2)
        along, across = jnp.where(odd == 0, dx, dy), jnp.where(odd == 0, dy, dx)
        return odd, along == 0, across == 0

    def sweep(start, copies):
        for copy in copies:
            copy.start() if start else copy.wait_send()

    def relay(t, b, start):
        odd, no_along, no_across = place(b)

        @pl.when(no_across)
        def _():
            sweep(start, [
                down(t, b, k, in_plane(k * odd, k * (1 - odd), core)) for k in far_first
            ])

        @pl.when(both(no_across, jnp.logical_not(no_along)))
        def _():
            sweep(start, [
                down(t, b, side + k, in_plane(k * odd, k * (1 - odd), 1 - core))
                for k in far_first
            ])

        @pl.when(no_along | no_across)
        def _():
            sweep(start, [down(t, b, 0, sibling)])

    def source(t, b, start):
        odd = lax.rem(b, 2)
        sweep(start, [
            down(t, b, side + k, in_plane(k * (1 - odd), k * odd, core)) for k in far_first
        ])

    def take_own(t, b):
        @pl.when(jnp.logical_not(is_source))
        def _():
            wait_block(t, b, core)
            relay(t, b, True)

    def multiply(t, group):
        mine = pl.ds(group * k, k)
        total = lag[mine] + dot(t + 1, group, near, core)

        @pl.when(t > 0)
        def _():
            for i in range(k):
                wait_block(t - 1, group * k + i, 1 - core)

        total = total + dot(t + 1, group, near, 1 - core)

        @pl.when(is_leaf)
        def _():
            snd[t, mine] = coded(total)
            for i in range(k):
                up(t, group * k + i).start()

        @pl.when(jnp.logical_not(is_leaf))
        def _():
            acc[mine] = total

    def wait_part(t, b, slot):
        pltpu.make_async_remote_copy(
            src_ref=snd.at[t, b], dst_ref=got.at[t, b, slot],
            send_sem=z_send.at[t, b], recv_sem=z_recv.at[t, b, slot],
            device_id=(parent_z, src), device_id_type=MESH,
        ).wait_recv()

    def behind(t, b):
        @pl.when(is_joint)
        def _():
            for slot, offset in enumerate((2, 1, -1, -2)):
                child = dist + offset

                @pl.when(both(child <= arm, (home == FAR) | (abs(offset) == 1)))
                def _(slot=slot):
                    wait_part(t, b, slot)
                    acc[b] += decoded(got[t, b, slot])

            snd[t, b] = coded(acc[b])
            up(t, b).start()

        @pl.when(is_root)
        def _():
            total = acc[b]
            for slot, least in ((1, 1), (0, FAR), (3, 1), (2, FAR)):
                if least <= (nz // 2 if slot < 2 else nz - nz // 2 - 1):
                    wait_part(t, b, slot)
                    total = total + decoded(got[t, b, slot])
            cur[t + 2, b, core] = jnp.tanh(inct[t, b].astype(jnp.float32) - total).astype(jnp.bfloat16)
            source(t, b, True)
            relay(t, b, True)

    passes = both(jnp.logical_not(is_source), (dx == 0) | (dy == 0))
    lead = jnp.where(passes, LEAD, 0)
    skew = jnp.where(both(passes, is_joint), SKEW, 0)

    def out_copies(t):
        return [
            pltpu.make_async_copy(
                cur.at[t + 2, :, h], out_ref.at[t, :, :, h * m : (h + 1) * m], out_sem.at[t, h]
            )
            for h in range(2)
        ]

    def step(t, carry):
        def turn(j, carry):
            @pl.when(both(t > 0, j < nb))
            def _():
                take_own(t - 1, j)

            at = j - lead

            @pl.when(both(at >= 0, at < nb, lax.rem(at, k) == k - 1))
            def _():
                multiply(t, at // k)

            @pl.when(both(jnp.logical_not(is_leaf), j >= skew, j - skew < nb))
            def _():
                behind(t, j - skew)

            return carry

        lax.fori_loop(0, 2 * nb, turn, 0)

        @pl.when(t > 0)
        def _():
            for copy in out_copies(t - 1):
                copy.start()

        @pl.when(t < steps - 1)
        def _():
            def refill(group, carry):
                lagged(t + 1, group)
                return carry

            lax.fori_loop(0, nb // k, refill, 0)

        return carry

    lax.fori_loop(0, steps, step, 0)

    def finish(b, carry):
        take_own(steps - 1, b)
        wait_block(steps - 1, b, 1 - core)
        return carry

    lax.fori_loop(0, nb, finish, 0)
    for copy in out_copies(steps - 1):
        copy.start()

    def drain(i, carry):
        t, b = i // nb, lax.rem(i, nb)
        relay(t, b, False)

        @pl.when(is_source)
        def _():
            source(t, b, False)

        @pl.when(jnp.logical_not(is_root))
        def _():
            up(t, b).wait_send()

        return carry

    lax.fori_loop(0, steps * nb, drain, 0)
    for t in range(steps):
        for copy in out_copies(t):
            copy.wait()


def per_device(delay_near, delay_far, incident, current_prev, current_prev2):
    steps, m, r = incident.shape
    nz = lax.axis_size("obs")
    side = math.isqrt(lax.axis_size("src") // 2)
    nb = BATCHES
    rb = r // nb
    rows = (nb, rb, 2 * m)
    blocks = pl.pallas_call(
        functools.partial(kernel, steps, nz, side),
        out_shape=jax.ShapeDtypeStruct((steps, *rows), jnp.bfloat16),
        in_specs=[pl.BlockSpec(memory_space=pl.ANY)] * 5,
        out_specs=pl.BlockSpec(memory_space=pl.ANY),
        scratch_shapes=[
            pltpu.VMEM((m, 2 * m), jnp.bfloat16),
            pltpu.VMEM((m, 2 * m), jnp.bfloat16),
            pltpu.VMEM((steps, nb, rb, m), jnp.bfloat16),
            pltpu.VMEM((steps + 2, nb, 2, rb, m), jnp.bfloat16),
            pltpu.VMEM((nb, rb, m), jnp.float32),
            pltpu.VMEM((nb, rb, m), jnp.float32),
            pltpu.VMEM((steps, nb, rb, m), jnp.bfloat16),
            pltpu.VMEM((steps, nb, 4, rb, m), jnp.bfloat16),
            pltpu.SemaphoreType.DMA((steps, nb)),
            pltpu.SemaphoreType.DMA((steps, nb, 4)),
            pltpu.SemaphoreType.DMA((steps, nb, 2 * side)),
            pltpu.SemaphoreType.DMA((steps, nb, 2)),
            pltpu.SemaphoreType.DMA((7,)),
            pltpu.SemaphoreType.DMA((steps, 2)),
        ],
        compiler_params=pltpu.CompilerParams(
            collective_id=0, has_side_effects=True, vmem_limit_bytes=VMEM
        ),
    )(
        delay_near,
        delay_far,
        incident.transpose(0, 2, 1).reshape(steps, nb, rb, m),
        current_prev.T.reshape(rows),
        current_prev2.T.reshape(rows),
    )
    return blocks.reshape(steps, r, 2 * m).transpose(0, 2, 1)


def solution(mesh):
    in_specs = (
        P("src", "obs"),
        P("src", "obs"),
        P(None, "src", None),
        P("obs", None),
        P("obs", None),
    )
    out_specs = P(None, "obs", None)
    return jax.shard_map(
        per_device, mesh=mesh, in_specs=in_specs, out_specs=out_specs, check_vma=False
    )
```

```python
import functools
import math

import jax
import jax.numpy as jnp
from jax import lax
from jax.experimental import pallas as pl
from jax.experimental.pallas import tpu as pltpu
from jax.sharding import PartitionSpec as P

BATCHES = 12
TOGETHER = 1
NEAR, FAR = 2, 6
SKEW = 2
VMEM = 60 * 1024 * 1024
LEAD = 1
MESH = pl.DeviceIdType.MESH


def both(*conds):
    return functools.reduce(jnp.logical_and, conds)


def coded(v):
    return (v * v * v * jnp.abs(v)).astype(jnp.bfloat16)


def decoded(c):
    c = c.astype(jnp.float32)
    size = lax.rsqrt(lax.rsqrt(jnp.abs(c) + 1e-36))
    return jnp.where(c < 0, -size, size)


def kernel(
    steps, nz, side, near_ref, far_ref, inc_ref, prev_ref, prev2_ref, out_ref,
    near, far, inct, cur, acc, lag, snd, got, z_send, z_recv, b_send, b_recv, in_sem, out_sem,
):
    nb, rb, m = acc.shape
    z = lax.axis_index("obs")
    src = lax.axis_index("src")
    core = lax.rem(src, 2)
    chip = src // 2
    x, y = chip // side, lax.rem(chip, side)

    rel = lax.rem(z - chip + nz, nz)
    upper = rel <= nz // 2
    dist = jnp.where(upper, rel, nz - rel)
    arm = jnp.where(upper, nz // 2, nz - nz // 2 - 1)
    is_root = rel == 0
    home = jnp.where(dist <= NEAR + 1, NEAR, FAR)
    apart = dist - home
    is_joint = both(jnp.logical_not(is_root), apart == 0)
    is_leaf = both(jnp.logical_not(is_root), apart != 0)
    to_root = (apart == 0) | (home > arm)
    hop = jnp.where(to_root, dist, apart)
    parent_z = lax.rem(jnp.where(upper, z - hop, z + hop) + nz, nz)
    root_slot = jnp.where(home == FAR, 0, 1) + jnp.where(upper, 0, 2)
    parent_slot = jnp.where(to_root, root_slot, jnp.where(apart > 0, 2 - apart, 1 - apart))

    rx, ry = z // side, lax.rem(z, side)
    dx = lax.rem(x - rx + side, side)
    dy = lax.rem(y - ry + side, side)
    is_source = both(dx == 0, dy == 0)
    sibling = (z, chip * 2 + 1 - core)

    far_first = sorted(range(1, side), key=lambda k: -min(k, side - k))

    on_x = {k: (lax.rem(x + k, side) * side + y) * 2 for k in far_first}
    on_y = {k: (x * side + lax.rem(y + k, side)) * 2 for k in far_first}

    def in_plane(swap, k, which):
        return (z, jnp.where(swap == 0, on_x[k], on_y[k]) + which)

    peers = [(z, on_axis[k] + c) for on_axis in (on_x, on_y) for k in far_first for c in range(2)]
    peers += [sibling]
    reach = sorted({k % nz for k in (-FAR, -2, -1, 1, 2, FAR)} - {0})
    peers += [(lax.rem(z + k, nz), src) for k in reach]
    barrier = pltpu.get_barrier_semaphore()
    for peer in peers:
        pl.semaphore_signal(barrier, inc=1, device_id=peer, device_id_type=MESH)

    def halves(ref, index):
        return [(ref.at[:, :, h * m : (h + 1) * m], cur.at[index, :, h]) for h in range(2)]

    loads = [(far_ref, far), *halves(prev2_ref, 0), (near_ref, near), *halves(prev_ref, 1)]
    loads = [pltpu.make_async_copy(*pair, in_sem.at[i]) for i, pair in enumerate(loads)]
    inc_load = pltpu.make_async_copy(inc_ref, inct, in_sem.at[6])
    for load in loads:
        load.start()

    @pl.when(is_root)
    def _():
        inc_load.start()

    k = TOGETHER

    def dot(index, first, count, ref, half):
        rows = cur[index, pl.ds(first, count), half].reshape(count * rb, m)
        cols = pl.ds(pl.multiple_of(half * m, m), m)
        field = lax.dot_general(
            rows, ref[:, cols], (((1,), (1,)), ((), ())), preferred_element_type=jnp.float32
        )
        return field.reshape(count, rb, m)

    def lagged(index):
        lag[...] = dot(index, 0, nb, far, 0) + dot(index, 0, nb, far, 1)

    for load in loads[:3]:
        load.wait()
    lagged(0)
    for load in loads[3:]:
        load.wait()

    @pl.when(is_root)
    def _():
        inc_load.wait()

    pl.semaphore_wait(barrier, len(peers))

    def up(t, b):
        return pltpu.make_async_remote_copy(
            src_ref=snd.at[t, b], dst_ref=got.at[t, b, parent_slot],
            send_sem=z_send.at[t, b], recv_sem=z_recv.at[t, b, parent_slot],
            device_id=(parent_z, src), device_id_type=MESH,
        )

    def down(t, b, which, device):
        return pltpu.make_async_remote_copy(
            src_ref=cur.at[t + 2, b, core], dst_ref=cur.at[t + 2, b, core],
            send_sem=b_send.at[t, b, which], recv_sem=b_recv.at[t, b, core],
            device_id=device, device_id_type=MESH,
        )

    def wait_block(t, b, half):
        pltpu.make_async_remote_copy(
            src_ref=cur.at[t + 2, b, half], dst_ref=cur.at[t + 2, b, half],
            send_sem=b_send.at[t, b, 0], recv_sem=b_recv.at[t, b, half],
            device_id=sibling, device_id_type=MESH,
        ).wait_recv()

    def place(b):
        odd = lax.rem(b, 2)
        along, across = jnp.where(odd == 0, dx, dy), jnp.where(odd == 0, dy, dx)
        return odd, along == 0, across == 0

    def sweep(start, copies):
        for copy in copies:
            copy.start() if start else copy.wait_send()

    def relay(t, b, start):
        odd, no_along, no_across = place(b)

        @pl.when(no_across)
        def _():
            sweep(start, [
                down(t, b, k, in_plane(1 - odd, k, core)) for k in far_first
            ])

        @pl.when(both(no_across, jnp.logical_not(no_along)))
        def _():
            sweep(start, [
                down(t, b, side + k, in_plane(1 - odd, k, 1 - core))
                for k in far_first
            ])

        @pl.when(no_along | no_across)
        def _():
            sweep(start, [down(t, b, 0, sibling)])

    def source(t, b, start):
        odd = lax.rem(b, 2)
        sweep(start, [
            down(t, b, side + k, in_plane(odd, k, core)) for k in far_first
        ])

    def take_own(t, b):
        @pl.when(jnp.logical_not(is_source))
        def _():
            wait_block(t, b, core)
            relay(t, b, True)

    def multiply(t, group):
        mine = pl.ds(group * k, k)
        @pl.when(t > 0)
        def _():
            for i in range(k):
                wait_block(t - 1, group * k + i, 1 - core)

        total = lag[mine] + dot(t + 1, group * k, k, near, 0) + dot(t + 1, group * k, k, near, 1)

        @pl.when(is_leaf)
        def _():
            snd[t, mine] = coded(total)
            for i in range(k):
                up(t, group * k + i).start()

        @pl.when(jnp.logical_not(is_leaf))
        def _():
            acc[mine] = total

    def wait_part(t, b, slot):
        pltpu.make_async_remote_copy(
            src_ref=snd.at[t, b], dst_ref=got.at[t, b, slot],
            send_sem=z_send.at[t, b], recv_sem=z_recv.at[t, b, slot],
            device_id=(parent_z, src), device_id_type=MESH,
        ).wait_recv()

    def behind(t, b):
        @pl.when(is_joint)
        def _():
            for slot, offset in enumerate((2, 1, -1, -2)):
                child = dist + offset

                @pl.when(both(child <= arm, (home == FAR) | (abs(offset) == 1)))
                def _(slot=slot):
                    wait_part(t, b, slot)
                    acc[b] += decoded(got[t, b, slot])

            snd[t, b] = coded(acc[b])
            up(t, b).start()

        @pl.when(is_root)
        def _():
            total = acc[b]
            for slot, least in ((1, 1), (0, FAR), (3, 1), (2, FAR)):
                if least <= (nz // 2 if slot < 2 else nz - nz // 2 - 1):
                    wait_part(t, b, slot)
                    total = total + decoded(got[t, b, slot])
            cur[t + 2, b, core] = jnp.tanh(inct[t, b].astype(jnp.float32) - total).astype(jnp.bfloat16)
            source(t, b, True)
            relay(t, b, True)

    passes = both(jnp.logical_not(is_source), (dx == 0) | (dy == 0))
    lead = jnp.where(passes, LEAD, 0)
    skew = jnp.where(both(passes, is_joint), SKEW, 0)

    def out_copies(t):
        return [
            pltpu.make_async_copy(
                cur.at[t + 2, :, h], out_ref.at[t, :, :, h * m : (h + 1) * m], out_sem.at[t, h]
            )
            for h in range(2)
        ]

    def step(t, carry):
        def turn(j, carry):
            @pl.when(both(t > 0, j < nb))
            def _():
                take_own(t - 1, j)

            at = j - lead

            @pl.when(both(at >= 0, at < nb, lax.rem(at, k) == k - 1))
            def _():
                multiply(t, at // k)

            @pl.when(both(jnp.logical_not(is_leaf), j >= skew, j - skew < nb))
            def _():
                behind(t, j - skew)

            return carry

        lax.fori_loop(0, 2 * nb, turn, 0)

        @pl.when(t > 0)
        def _():
            for copy in out_copies(t - 1):
                copy.start()

        @pl.when(t < steps - 1)
        def _():
            lagged(t + 1)

        return carry

    lax.fori_loop(0, steps, step, 0)

    def finish(b, carry):
        take_own(steps - 1, b)
        wait_block(steps - 1, b, 1 - core)
        return carry

    lax.fori_loop(0, nb, finish, 0)
    for copy in out_copies(steps - 1):
        copy.start()

    def drain(i, carry):
        t, b = i // nb, lax.rem(i, nb)
        relay(t, b, False)

        @pl.when(is_source)
        def _():
            source(t, b, False)

        @pl.when(jnp.logical_not(is_root))
        def _():
            up(t, b).wait_send()

        return carry

    lax.fori_loop(0, steps * nb, drain, 0)
    for t in range(steps):
        for copy in out_copies(t):
            copy.wait()


def per_device(delay_near, delay_far, incident, current_prev, current_prev2):
    steps, m, r = incident.shape
    nz = lax.axis_size("obs")
    side = math.isqrt(lax.axis_size("src") // 2)
    nb = BATCHES
    rb = r // nb
    rows = (nb, rb, 2 * m)
    blocks = pl.pallas_call(
        functools.partial(kernel, steps, nz, side),
        out_shape=jax.ShapeDtypeStruct((steps, *rows), jnp.bfloat16),
        in_specs=[pl.BlockSpec(memory_space=pl.ANY)] * 5,
        out_specs=pl.BlockSpec(memory_space=pl.ANY),
        scratch_shapes=[
            pltpu.VMEM((m, 2 * m), jnp.bfloat16),
            pltpu.VMEM((m, 2 * m), jnp.bfloat16),
            pltpu.VMEM((steps, nb, rb, m), jnp.bfloat16),
            pltpu.VMEM((steps + 2, nb, 2, rb, m), jnp.bfloat16),
            pltpu.VMEM((nb, rb, m), jnp.float32),
            pltpu.VMEM((nb, rb, m), jnp.float32),
            pltpu.VMEM((steps, nb, rb, m), jnp.bfloat16),
            pltpu.VMEM((steps, nb, 4, rb, m), jnp.bfloat16),
            pltpu.SemaphoreType.DMA((steps, nb)),
            pltpu.SemaphoreType.DMA((steps, nb, 4)),
            pltpu.SemaphoreType.DMA((steps, nb, 2 * side)),
            pltpu.SemaphoreType.DMA((steps, nb, 2)),
            pltpu.SemaphoreType.DMA((7,)),
            pltpu.SemaphoreType.DMA((steps, 2)),
        ],
        compiler_params=pltpu.CompilerParams(
            collective_id=0, has_side_effects=True, vmem_limit_bytes=VMEM
        ),
    )(
        delay_near,
        delay_far,
        incident.transpose(0, 2, 1).reshape(steps, nb, rb, m),
        current_prev.T.reshape(rows),
        current_prev2.T.reshape(rows),
    )
    return blocks.reshape(steps, r, 2 * m).transpose(0, 2, 1)


def solution(mesh):
    in_specs = (
        P("src", "obs"),
        P("src", "obs"),
        P(None, "src", None),
        P("obs", None),
        P("obs", None),
    )
    out_specs = P(None, "obs", None)
    return jax.shard_map(
        per_device, mesh=mesh, in_specs=in_specs, out_specs=out_specs, check_vma=False
    )
```
